32 devices in a mesh: clip: 2 (over core), tm: 16 (over z, y, x).
Axes of the slice: x: 2, y: 2, z: 4, core: 2. Of those that a mesh axis runs over, the one named last changes fastest.
Arguments:
- clip_frames: bfloat16 [2, 32, 64, 64, 128], P('clip', 'tm'), may hold values from -6 to 6
- spatial_weight: bfloat16 [3, 3, 128, 256], replicated, may hold values from -0.1875 to 0.1875
- norm_gain: float32 [256], replicated, may hold values from 0.5 to 1.5
- norm_bias: float32 [256], replicated, may hold values from -3 to 3
- temporal_weight: bfloat16 [3, 256, 256], replicated, may hold values from -0.21875 to 0.21875
- cotangent: bfloat16 [2, 32, 32, 32, 256], P('clip', 'tm'), may hold values from -0.0234375 to 0.0234375
Outputs:
- mixed: bfloat16 [2, 32, 32, 32, 256], P('clip', 'tm')
- spatial_grad: float32 [3, 3, 128, 256], replicated
- gain_grad: float32 [256], replicated
- bias_grad: float32 [256], replicated
- temporal_grad: float32 [3, 256, 256], replicated
The draws below stay inside these ranges and needn't reach their ends.
All inputs are finite; a program needn't handle non-finite values.
Results may differ from the reference program's by a relative error of at most 0.0085.
Values may be sent and summed in bfloat16 or wider, within the bound.
A program may use at most 64 MiB of HBM per device.

```python
import jax
import jax.numpy as jnp
from jax import lax

C1 = 128
C2 = 256
GROUPS = 32
DILATION_FRAMES = 4
HEIGHT = 64
WIDTH = 64
CLIPS = 2
FRAMES = 32
H2 = 32
W2 = 32


def block_scale(key, extent, shards, low, top_value):
    factor_of = 1.0
    for position, shards_of in shards:
        heights = jax.random.uniform(jax.random.fold_in(jax.random.fold_in(key, 6), position), (shards_of,), jnp.float32, low / len(shards), top_value / len(shards))
        factor_of = factor_of * jnp.repeat(jnp.exp(heights), extent[position] // shards_of).reshape((-1,) + (1,) * (len(extent) - 1 - position))
    return factor_of


def scatter_about(stream_key, extent, scale, reach, cuts=(), kind=jnp.bfloat16):
    loudness = block_scale(stream_key, extent, cuts, -0.22, 0.18) if cuts else 1.0
    values = jax.random.normal(stream_key, extent, jnp.float32) * scale * loudness
    return jnp.minimum(jnp.maximum(values, -reach), reach).astype(kind)


def setup_inputs(seed: int = 0) -> dict:
    streams_of = jax.random.split(jax.random.key(seed), 7)
    return {
        "clip_frames": scatter_about(streams_of[0], (CLIPS, FRAMES, HEIGHT, WIDTH, C1), 1.0, 6.0, ((0, 2), (1, 16))),
        "spatial_weight": scatter_about(streams_of[1], (3, 3, C1, C2), (9 * C1) ** -0.5, 0.1875),
        "norm_gain": jnp.clip(1.0 + 0.1 * jax.random.normal(streams_of[2], (C2,), jnp.float32), 0.5, 1.5),
        "norm_bias": scatter_about(streams_of[3], (C2,), 0.5, 3.0, (), jnp.float32),
        "temporal_weight": scatter_about(streams_of[4], (3, C2, C2), (3 * C2) ** -0.5, 0.21875),
        "cotangent": scatter_about(streams_of[5], (CLIPS, FRAMES, H2, W2, C2), (1.0 / (CLIPS * FRAMES * H2 * W2) ** 0.5), 0.0234375, ((0, 2), (1, 16))),
    }


epsilon = 1e-05

def gather_patches(frames_in):
    height = frames_in.shape[1]
    width = frames_in.shape[2]
    padded = jnp.pad(frames_in, ((0, 0), (1, 1), (1, 1), (0, 0)))
    pieces = []
    for row_offset in range(3):
        for col_offset in range(3):
            pieces.append(padded[:, row_offset:row_offset + height:2, col_offset:col_offset + width:2, :])
    return jnp.concatenate(pieces, axis=-1)

def activate(conv_out, gain, bias):
    grouped = conv_out.reshape(conv_out.shape[:-1] + (GROUPS, conv_out.shape[-1] // GROUPS))
    center = lax.optimization_barrier(jnp.mean(grouped, axis=(1, 2, 4), keepdims=True))
    temporal_reach = lax.optimization_barrier(jnp.mean((grouped - center) ** 2, axis=(1, 2, 4), keepdims=True))
    normed = ((grouped - center) * lax.rsqrt(temporal_reach + epsilon)).reshape(conv_out.shape)
    return jax.nn.silu(normed * gain + bias)

def padded_lag(values, frame_offset):
    if frame_offset == 0:
        return values
    frames = values.shape[0]
    if frame_offset > 0:
        filler = jnp.zeros((frame_offset,) + values.shape[1:], values.dtype)
        return jnp.concatenate([filler, values[:frames - frame_offset]], axis=0)
    filler = jnp.zeros((-frame_offset,) + values.shape[1:], values.dtype)
    return jnp.concatenate([values[-frame_offset:], filler], axis=0)

def temporal_pass(acts, grads, weight):
    chans = acts.shape[-1]
    total = acts.astype(jnp.float32)
    backward_total_sum = grads.astype(jnp.float32)
    tap_grads = []
    flattened_gradients = grads.reshape(-1, chans)
    for kernel_tap_index in range(3):
        frame_offset = kernel_tap_index * DILATION_FRAMES
        earlier = padded_lag(acts, frame_offset).reshape(-1, chans)
        later = padded_lag(grads, -frame_offset).reshape(-1, chans)
        total = total + jnp.dot(earlier, weight[kernel_tap_index], preferred_element_type=jnp.float32).reshape(acts.shape)
        backward_total_sum = backward_total_sum + jnp.dot(later, weight[kernel_tap_index].T, preferred_element_type=jnp.float32).reshape(acts.shape)
        tap_grads.append(lax.dot_general(earlier, flattened_gradients, (((0,), (0,)), ((), ())), preferred_element_type=jnp.float32))
    return (total.astype(jnp.bfloat16), backward_total_sum.astype(jnp.bfloat16), jnp.stack(tap_grads))

def reference(clip_frames, spatial_weight, norm_gain, norm_bias, temporal_weight, cotangent):
    kernel = spatial_weight.reshape(-1, spatial_weight.shape[-1])

    def one_clip(pair):
        frames_in, upstream = pair
        patches = gather_patches(frames_in)
        flat = patches.reshape(-1, patches.shape[-1])
        out_shape = patches.shape[:-1] + (kernel.shape[1],)
        conv_out = jnp.dot(flat, kernel, preferred_element_type=jnp.float32).reshape(out_shape)
        activated, pullback = jax.vjp(activate, conv_out, norm_gain, norm_bias)
        acts = activated.astype(jnp.bfloat16)
        mixed, act_grad, temporal_part = temporal_pass(acts, upstream, temporal_weight)
        conv_grad, gain_partial_sum, bias_part = pullback(act_grad.astype(jnp.float32))
        conv_grad = conv_grad.astype(jnp.bfloat16).reshape(-1, kernel.shape[1])
        spatial_part = lax.dot_general(flat, conv_grad, (((0,), (0,)), ((), ())), preferred_element_type=jnp.float32)
        return (mixed, spatial_part, gain_partial_sum, bias_part, temporal_part)
    results = lax.map(one_clip, (clip_frames, cotangent))
    spatial_grad = lax.optimization_barrier(jnp.sum(results[1], axis=0)).reshape(spatial_weight.shape)
    return (results[0], spatial_grad, lax.optimization_barrier(jnp.sum(results[2], axis=0)), lax.optimization_barrier(jnp.sum(results[3], axis=0)), lax.optimization_barrier(jnp.sum(results[4], axis=0)))
```

```python
import functools

import jax
import jax.numpy as jnp
from jax import lax
from jax.experimental import pallas as pl
from jax.experimental.pallas import tpu as pltpu
from jax.sharding import PartitionSpec as P

GROUPS = 32
DILATION_FRAMES = 4


epsilon = 1e-05


def delay_rows(values):
    return jnp.pad(values, ((0, 0), (1, 0), (0, 0), (0, 0)))[:, :-1]


def delay_cols(values):
    return jnp.pad(values, ((0, 0), (0, 0), (1, 0), (0, 0)))[:, :, :-1]


def advance_rows(values):
    return jnp.pad(values, ((0, 0), (0, 1), (0, 0), (0, 0)))[:, 1:]


def advance_cols(values):
    return jnp.pad(values, ((0, 0), (0, 0), (0, 1), (0, 0)))[:, :, 1:]


def split_phases(frames_in):
    frames, height, width, chans = frames_in.shape
    viewed = frames_in.reshape(frames, height // 2, 2, width // 2, 2, chans)
    phases = {}
    for row_phase in range(2):
        for col_phase in range(2):
            phases[row_phase, col_phase] = viewed[:, :, row_phase, :, col_phase, :].reshape(
                -1, chans
            )
    return phases


def tap_layout(offset):
    return (0 if offset == 1 else 1, offset == 0)


def membership(chans):
    channel_group = lax.broadcasted_iota(jnp.int32, (chans, GROUPS), 0) // (chans // GROUPS)
    group_index = lax.broadcasted_iota(jnp.int32, (chans, GROUPS), 1)
    return (channel_group == group_index).astype(jnp.float32)


def activate(conv_out, gain, bias):
    chans = conv_out.shape[-1]
    member = membership(chans)
    count = conv_out.shape[1] * conv_out.shape[2] * (chans // GROUPS)
    high = lax.Precision.HIGHEST
    chan_sum = jnp.sum(conv_out, axis=(1, 2))
    group_mean = jnp.dot(chan_sum, member, precision=high) / count
    center = jnp.dot(group_mean, member.T, precision=high)
    deviation = conv_out - center[:, None, None, :]
    chan_square = jnp.sum(deviation * deviation, axis=(1, 2))
    group_var = jnp.dot(chan_square, member, precision=high) / count
    scaling = jnp.dot(lax.rsqrt(group_var + epsilon), member.T, precision=high)
    normed = deviation * scaling[:, None, None, :]
    return jax.nn.silu(normed * gain + bias)


def from_device(values, offset, tm_size):
    pairs = [(src, src + offset) for src in range(tm_size) if 0 <= src + offset < tm_size]
    return lax.ppermute(values, "tm", pairs)


def bit_steps(clip_size, tm_size):
    steps = [("clip", 1)] if clip_size > 1 else []
    steps += [("tm", 1 << k) for k in range(tm_size.bit_length() - 1)]
    steps += [("clip", 1 << k) for k in range(1, clip_size.bit_length() - 1)]
    return steps


def sum_kernel(steps, x_ref, out_ref, acc, outgoing, incoming, rs_send, rs_recv, ag_send, ag_recv):
    place = {"clip": lax.axis_index("clip"), "tm": lax.axis_index("tm")}
    bits, partners = [], []
    for axis, weight in steps:
        bit = (place[axis] // weight) % 2
        other = place[axis] + weight * (1 - 2 * bit)
        bits.append(bit)
        partners.append((other, place["tm"]) if axis == "clip" else (place["clip"], other))

    barrier = pltpu.get_barrier_semaphore()
    for partner in partners:
        pl.semaphore_signal(
            barrier, inc=1, device_id=partner, device_id_type=pl.DeviceIdType.MESH
        )
    pl.semaphore_wait(barrier, len(partners))

    base = 0
    half = x_ref.shape[0] // 2
    offset = 0
    bases = []
    copies = []
    for step, partner in enumerate(partners):
        source = x_ref if step == 0 else acc
        keep = base + bits[step] * half
        give = base + (1 - bits[step]) * half
        slot = pl.ds(offset, half)
        outgoing[slot] = source[pl.ds(give, half)].astype(jnp.bfloat16)
        copy = pltpu.make_async_remote_copy(
            src_ref=outgoing.at[slot],
            dst_ref=incoming.at[slot],
            send_sem=rs_send.at[step],
            recv_sem=rs_recv.at[step],
            device_id=partner,
            device_id_type=pl.DeviceIdType.MESH,
        )
        copy.start()
        copies.append(copy)
        copy.wait_recv()
        acc[pl.ds(keep, half)] = source[pl.ds(keep, half)] + incoming[slot].astype(jnp.float32)
        bases.append(keep)
        base = keep
        offset += half
        half //= 2

    out_ref[pl.ds(base, 1)] = acc[pl.ds(base, 1)].astype(jnp.bfloat16)
    size = 1
    for step in reversed(range(len(partners))):
        held = out_ref.at[pl.ds(bases[step], size)]
        copy = pltpu.make_async_remote_copy(
            src_ref=held,
            dst_ref=held,
            send_sem=ag_send.at[step],
            recv_sem=ag_recv.at[step],
            device_id=partners[step],
            device_id_type=pl.DeviceIdType.MESH,
        )
        copy.start()
        copies.append(copy)
        copy.wait_recv()
        size *= 2
    for copy in copies:
        copy.wait_send()


def sum_everywhere(values, clip_size, tm_size):
    devices = clip_size * tm_size
    steps = bit_steps(clip_size, tm_size)
    rows, chans = values.shape
    unit = 8 * devices
    padded = -(-rows // unit) * unit
    values = jnp.pad(values, ((0, padded - rows), (0, 0)))
    shape = (devices, padded // devices, chans)
    total = pl.pallas_call(
        functools.partial(sum_kernel, steps),
        out_shape=jax.ShapeDtypeStruct(shape, jnp.bfloat16),
        in_specs=[pl.BlockSpec(memory_space=pltpu.VMEM)],
        out_specs=pl.BlockSpec(memory_space=pltpu.VMEM),
        scratch_shapes=[
            pltpu.VMEM(shape, jnp.float32),
            pltpu.VMEM(shape, jnp.bfloat16),
            pltpu.VMEM(shape, jnp.bfloat16),
        ]
        + [pltpu.SemaphoreType.DMA((len(steps),))] * 4,
        compiler_params=pltpu.CompilerParams(
            collective_id=0, has_side_effects=True, vmem_limit_bytes=32 * 1024 * 1024
        ),
    )(values.reshape(shape))
    return total.astype(jnp.float32).reshape(padded, chans)[:rows]


def per_device(clip_size, tm_size, clip_frames, spatial_weight, norm_gain, norm_bias, temporal_weight, cotangent):
    frames_in = clip_frames[0]
    upstream = cotangent[0]
    frames, height, width, _ = frames_in.shape
    out_chans = spatial_weight.shape[-1]
    out_shape = (frames, height // 2, width // 2, out_chans)
    phases = split_phases(frames_in)
    partial_sums = {}
    for row_offset in range(3):
        row_phase, row_delay = tap_layout(row_offset)
        for col_offset in range(3):
            col_phase, col_delay = tap_layout(col_offset)
            product = jnp.dot(
                phases[row_phase, col_phase],
                spatial_weight[row_offset, col_offset],
                preferred_element_type=jnp.float32,
            )
            key_pair = (row_delay, col_delay)
            if key_pair in partial_sums:
                partial_sums[key_pair] = partial_sums[key_pair] + product
            else:
                partial_sums[key_pair] = product
    conv_out = partial_sums[False, False].reshape(out_shape)
    conv_out = conv_out + delay_rows(partial_sums[True, False].reshape(out_shape))
    conv_out = conv_out + delay_cols(partial_sums[False, True].reshape(out_shape))
    conv_out = conv_out + delay_rows(delay_cols(partial_sums[True, True].reshape(out_shape)))
    activated, pullback = jax.vjp(activate, conv_out, norm_gain, norm_bias)
    acts = activated.astype(jnp.bfloat16)
    flat_acts = acts.reshape(-1, out_chans)
    mixed_sum = flat_acts.astype(jnp.float32)
    act_grad_sum = upstream.reshape(-1, out_chans).astype(jnp.float32)
    tap_grads = []
    for tap in range(3):
        hop = tap * DILATION_FRAMES // frames
        earlier = from_device(acts, hop, tm_size) if tap else acts
        later = from_device(upstream, -hop, tm_size) if tap else upstream
        earlier = earlier.reshape(-1, out_chans)
        later = later.reshape(-1, out_chans)
        mixed_sum = mixed_sum + jnp.dot(
            earlier, temporal_weight[tap], preferred_element_type=jnp.float32
        )
        act_grad_sum = act_grad_sum + jnp.dot(
            later, temporal_weight[tap].T, preferred_element_type=jnp.float32
        )
        tap_grads.append(
            lax.dot_general(
                flat_acts, later, (((0,), (0,)), ((), ())), preferred_element_type=jnp.float32
            )
        )
    mixed = mixed_sum.astype(jnp.bfloat16).reshape(out_shape)
    act_grad = act_grad_sum.astype(jnp.bfloat16).reshape(out_shape)
    conv_grad, gain_partial_sum, bias_part = pullback(act_grad.astype(jnp.float32))
    conv_grad = conv_grad.astype(jnp.bfloat16)
    grad_versions = {
        (False, False): conv_grad.reshape(-1, out_chans),
        (True, False): advance_rows(conv_grad).reshape(-1, out_chans),
        (False, True): advance_cols(conv_grad).reshape(-1, out_chans),
        (True, True): advance_rows(advance_cols(conv_grad)).reshape(-1, out_chans),
    }
    parts = []
    for row_offset in range(3):
        row_phase, row_delay = tap_layout(row_offset)
        for col_offset in range(3):
            col_phase, col_delay = tap_layout(col_offset)
            parts.append(
                lax.dot_general(
                    phases[row_phase, col_phase],
                    grad_versions[row_delay, col_delay],
                    (((0,), (0,)), ((), ())),
                    preferred_element_type=jnp.float32,
                )
            )
    spatial_rows = 9 * spatial_weight.shape[2]
    parts += tap_grads + [gain_partial_sum[None], bias_part[None]]
    totals = sum_everywhere(jnp.concatenate(parts), clip_size, tm_size)
    spatial_gradient_total = totals[:spatial_rows].reshape(spatial_weight.shape)
    temporal_total = totals[spatial_rows : spatial_rows + 3 * out_chans].reshape(
        temporal_weight.shape
    )
    gain_total = totals[spatial_rows + 3 * out_chans]
    bias_total = totals[spatial_rows + 3 * out_chans + 1]
    return (mixed[None], spatial_gradient_total, gain_total, bias_total, temporal_total)


def solution(mesh):
    return jax.shard_map(
        functools.partial(per_device, mesh.shape["clip"], mesh.shape["tm"]),
        mesh=mesh,
        in_specs=(
            P("clip", "tm", None, None, None),
            P(),
            P(),
            P(),
            P(),
            P("clip", "tm", None, None, None),
        ),
        out_specs=(P("clip", "tm", None, None, None), P(), P(), P(), P()),
        check_vma=False,
    )
```

```python
import functools

import jax
import jax.numpy as jnp
from jax import lax
from jax.experimental import pallas as pl
from jax.experimental.pallas import tpu as pltpu
from jax.sharding import PartitionSpec as P

GROUPS = 32
DILATION_FRAMES = 4


epsilon = 1e-05


def delay_rows(values):
    return jnp.pad(values, ((0, 0), (1, 0), (0, 0), (0, 0)))[:, :-1]


def delay_cols(values):
    return jnp.pad(values, ((0, 0), (0, 0), (1, 0), (0, 0)))[:, :, :-1]


def advance_rows(values):
    return jnp.pad(values, ((0, 0), (0, 1), (0, 0), (0, 0)))[:, 1:]


def advance_cols(values):
    return jnp.pad(values, ((0, 0), (0, 0), (0, 1), (0, 0)))[:, :, 1:]


def split_phases(frames_in):
    frames, height, width, chans = frames_in.shape
    viewed = frames_in.reshape(frames, height // 2, 2, width // 2, 2, chans)
    phases = {}
    for row_phase in range(2):
        for col_phase in range(2):
            phases[row_phase, col_phase] = viewed[:, :, row_phase, :, col_phase, :].reshape(
                -1, chans
            )
    return phases


def tap_layout(offset):
    return (0 if offset == 1 else 1, offset == 0)


def membership(chans):
    channel_group = lax.broadcasted_iota(jnp.int32, (chans, GROUPS), 0) // (chans // GROUPS)
    group_index = lax.broadcasted_iota(jnp.int32, (chans, GROUPS), 1)
    return (channel_group == group_index).astype(jnp.float32)


def activate(conv_out, gain, bias):
    chans = conv_out.shape[-1]
    member = membership(chans)
    count = conv_out.shape[1] * conv_out.shape[2] * (chans // GROUPS)
    high = lax.Precision.HIGHEST
    chan_sum = jnp.sum(conv_out, axis=(1, 2))
    group_mean = jnp.dot(chan_sum, member, precision=high) / count
    center = jnp.dot(group_mean, member.T, precision=high)
    deviation = conv_out - center[:, None, None, :]
    chan_square = jnp.sum(deviation * deviation, axis=(1, 2))
    group_var = jnp.dot(chan_square, member, precision=high) / count
    scaling = jnp.dot(lax.rsqrt(group_var + epsilon), member.T, precision=high)
    normed = deviation * scaling[:, None, None, :]
    return jax.nn.silu(normed * gain + bias)


def from_device(values, offset, tm_size):
    pairs = [(src, src + offset) for src in range(tm_size) if 0 <= src + offset < tm_size]
    return lax.ppermute(values, "tm", pairs)


def bit_steps(clip_size, tm_size):
    steps = [("clip", 1)] if clip_size > 1 else []
    steps += [("tm", 1 << k) for k in range(tm_size.bit_length() - 1)]
    steps += [("clip", 1 << k) for k in range(1, clip_size.bit_length() - 1)]
    return steps


STREAMS = 2


def sum_kernel(steps, sizes, *refs):
    parts, refs = refs[: len(sizes)], refs[len(sizes) :]
    out_ref, acc, outgoing, incoming, rs_send, rs_recv, ag_send, ag_recv = refs
    place = {"clip": lax.axis_index("clip"), "tm": lax.axis_index("tm")}
    bits, partners = [], []
    for axis, weight in steps:
        bit = (place[axis] // weight) % 2
        other = place[axis] + weight * (1 - 2 * bit)
        bits.append(bit)
        partners.append((other, place["tm"]) if axis == "clip" else (place["clip"], other))

    barrier = pltpu.get_barrier_semaphore()
    for partner in partners:
        pl.semaphore_signal(
            barrier, inc=1, device_id=partner, device_id_type=pl.DeviceIdType.MESH
        )

    _, devices, unit, chans = acc.shape
    flat = acc.reshape(STREAMS * devices * unit, chans)
    row = 0
    for part, size in zip(parts, sizes):
        flat[row : row + size] = part[...].reshape(size, chans)
        row += size
    flat[row:] = jnp.zeros((flat.shape[0] - row, chans), jnp.float32)
    pl.semaphore_wait(barrier, len(partners))

    count = len(steps)
    orders = [list(range(count)) for _ in range(STREAMS)]
    if count > 2:
        orders[1][1], orders[1][2] = 2, 1
    base = [0] * STREAMS
    kept = [[] for _ in range(STREAMS)]
    flying = [None] * STREAMS
    copies = []

    def send_half(stream, turn):
        which = orders[stream][turn]
        half = devices >> (turn + 1)
        slot = pl.ds(devices - 2 * half, half)
        give = base[stream] + (1 - bits[which]) * half
        outgoing[stream, slot] = acc[stream, pl.ds(give, half)].astype(jnp.bfloat16)
        copy = pltpu.make_async_remote_copy(
            src_ref=outgoing.at[stream, slot],
            dst_ref=incoming.at[stream, slot],
            send_sem=rs_send.at[stream, turn],
            recv_sem=rs_recv.at[stream, turn],
            device_id=partners[which],
            device_id_type=pl.DeviceIdType.MESH,
        )
        copy.start()
        copies.append(copy)
        flying[stream] = copy

    def add_half(stream, turn):
        which = orders[stream][turn]
        half = devices >> (turn + 1)
        slot = pl.ds(devices - 2 * half, half)
        keep = base[stream] + bits[which] * half
        flying[stream].wait_recv()
        acc[stream, pl.ds(keep, half)] += incoming[stream, slot].astype(jnp.float32)
        kept[stream].append(keep)
        base[stream] = keep

    def send_held(stream, turn):
        which = orders[stream][turn]
        held = out_ref.at[stream, pl.ds(kept[stream][turn], devices >> (turn + 1))]
        copy = pltpu.make_async_remote_copy(
            src_ref=held,
            dst_ref=held,
            send_sem=ag_send.at[stream, turn],
            recv_sem=ag_recv.at[stream, turn],
            device_id=partners[which],
            device_id_type=pl.DeviceIdType.MESH,
        )
        copy.start()
        copies.append(copy)
        flying[stream] = copy

    for stream in range(STREAMS):
        send_half(stream, 0)
    for turn in range(count):
        for stream in range(STREAMS):
            add_half(stream, turn)
            if turn + 1 < count:
                send_half(stream, turn + 1)
            else:
                own = pl.ds(base[stream], 1)
                out_ref[stream, own] = acc[stream, own].astype(jnp.bfloat16)
                send_held(stream, turn)
    for turn in reversed(range(count)):
        for stream in range(STREAMS):
            flying[stream].wait_recv()
            if turn > 0:
                send_held(stream, turn - 1)
    for copy in copies:
        copy.wait_send()


def sum_everywhere(parts, clip_size, tm_size):
    devices = clip_size * tm_size
    steps = bit_steps(clip_size, tm_size)
    chans = parts[0].shape[-1]
    sizes = tuple(part.shape[0] for part in parts)
    unit = -(-sum(sizes) // (STREAMS * devices * 8)) * 8
    shape = (STREAMS, devices, unit, chans)
    total = pl.pallas_call(
        functools.partial(sum_kernel, steps, sizes),
        out_shape=jax.ShapeDtypeStruct(shape, jnp.bfloat16),
        in_specs=[pl.BlockSpec(memory_space=pltpu.VMEM)] * len(parts),
        out_specs=pl.BlockSpec(memory_space=pltpu.VMEM),
        scratch_shapes=[
            pltpu.VMEM(shape, jnp.float32),
            pltpu.VMEM(shape, jnp.bfloat16),
            pltpu.VMEM(shape, jnp.bfloat16),
        ]
        + [pltpu.SemaphoreType.DMA((STREAMS, len(steps)))] * 4,
        compiler_params=pltpu.CompilerParams(
            collective_id=0, has_side_effects=True, vmem_limit_bytes=32 * 1024 * 1024
        ),
    )(*parts)
    return total.reshape(-1, chans).astype(jnp.float32)


def later_frames(upstream, hop, tm_size):
    upper = (lax.axis_index("tm") // hop) % 2 == 1
    lows = [place for place in range(tm_size) if place // hop % 2 == 0]
    far = [from_device(block, -2 * hop, tm_size) for block in upstream]
    own = lax.ppermute(upstream, "tm", [(low + hop, low) for low in lows])
    passed = [lax.ppermute(block, "tm", [(low, low + hop) for low in lows]) for block in far]
    near = [jnp.where(upper, passed[k], own[k]) for k in range(len(far))]
    return jnp.stack(near), jnp.stack(far)


def per_device(clip_size, tm_size, clip_frames, spatial_weight, norm_gain, norm_bias, temporal_weight, cotangent):
    frames_in = clip_frames[0]
    upstream = cotangent[0]
    frames, height, width, _ = frames_in.shape
    out_chans = spatial_weight.shape[-1]
    out_shape = (frames, height // 2, width // 2, out_chans)
    phases = split_phases(frames_in)
    partial_sums = {}
    for row_offset in range(3):
        row_phase, row_delay = tap_layout(row_offset)
        for col_offset in range(3):
            col_phase, col_delay = tap_layout(col_offset)
            product = jnp.dot(
                phases[row_phase, col_phase],
                spatial_weight[row_offset, col_offset],
                preferred_element_type=jnp.float32,
            )
            key_pair = (row_delay, col_delay)
            if key_pair in partial_sums:
                partial_sums[key_pair] = partial_sums[key_pair] + product
            else:
                partial_sums[key_pair] = product
    conv_out = partial_sums[False, False].reshape(out_shape)
    conv_out = conv_out + delay_rows(partial_sums[True, False].reshape(out_shape))
    conv_out = conv_out + delay_cols(partial_sums[False, True].reshape(out_shape))
    conv_out = conv_out + delay_rows(delay_cols(partial_sums[True, True].reshape(out_shape)))
    activated, pullback = jax.vjp(activate, conv_out, norm_gain, norm_bias)
    acts = activated.astype(jnp.bfloat16)
    flat_acts = acts.reshape(-1, out_chans)
    mixed_sum = flat_acts.astype(jnp.float32)
    act_grad_sum = upstream.reshape(-1, out_chans).astype(jnp.float32)
    tap_grads = []
    hop = DILATION_FRAMES // frames
    near, far = later_frames(upstream, hop, tm_size)
    far_acts = from_device(acts, 2 * hop, tm_size)
    upstream, near, far, far_acts = lax.optimization_barrier((upstream, near, far, far_acts))
    upper = (lax.axis_index("tm") // hop) % 2 == 1
    near_acts = lax.ppermute(
        jnp.where(upper, far_acts, acts), "tm", [(src, src ^ hop) for src in range(tm_size)]
    )
    for tap in range(3):
        earlier = (acts, near_acts, far_acts)[tap]
        later = (upstream, near, far)[tap]
        earlier = earlier.reshape(-1, out_chans)
        later = later.reshape(-1, out_chans)
        mixed_sum = mixed_sum + jnp.dot(
            earlier, temporal_weight[tap], preferred_element_type=jnp.float32
        )
        act_grad_sum = act_grad_sum + jnp.dot(
            later, temporal_weight[tap].T, preferred_element_type=jnp.float32
        )
        tap_grads.append(
            lax.dot_general(
                flat_acts, later, (((0,), (0,)), ((), ())), preferred_element_type=jnp.float32
            )
        )
    mixed = mixed_sum.astype(jnp.bfloat16).reshape(out_shape)
    act_grad = act_grad_sum.astype(jnp.bfloat16).reshape(out_shape)
    conv_grad, gain_partial_sum, bias_part = pullback(act_grad.astype(jnp.float32))
    conv_grad = conv_grad.astype(jnp.bfloat16)
    grad_versions = {
        (False, False): conv_grad.reshape(-1, out_chans),
        (True, False): advance_rows(conv_grad).reshape(-1, out_chans),
        (False, True): advance_cols(conv_grad).reshape(-1, out_chans),
        (True, True): advance_rows(advance_cols(conv_grad)).reshape(-1, out_chans),
    }
    parts = []
    for row_offset in range(3):
        row_phase, row_delay = tap_layout(row_offset)
        for col_offset in range(3):
            col_phase, col_delay = tap_layout(col_offset)
            parts.append(
                lax.dot_general(
                    phases[row_phase, col_phase],
                    grad_versions[row_delay, col_delay],
                    (((0,), (0,)), ((), ())),
                    preferred_element_type=jnp.float32,
                )
            )
    spatial_rows = 9 * spatial_weight.shape[2]
    parts += tap_grads
    parts.append(jnp.stack([gain_partial_sum, bias_part]))
    totals = sum_everywhere(parts, clip_size, tm_size)
    spatial_gradient_total = totals[:spatial_rows].reshape(spatial_weight.shape)
    temporal_total = totals[spatial_rows : spatial_rows + 3 * out_chans].reshape(
        temporal_weight.shape
    )
    gain_total = totals[spatial_rows + 3 * out_chans]
    bias_total = totals[spatial_rows + 3 * out_chans + 1]
    return (mixed[None], spatial_gradient_total, gain_total, bias_total, temporal_total)


def solution(mesh):
    return jax.shard_map(
        functools.partial(per_device, mesh.shape["clip"], mesh.shape["tm"]),
        mesh=mesh,
        in_specs=(
            P("clip", "tm", None, None, None),
            P(),
            P(),
            P(),
            P(),
            P("clip", "tm", None, None, None),
        ),
        out_specs=(P("clip", "tm", None, None, None), P(), P(), P(), P()),
        check_vma=False,
    )
```

```python
import functools

import jax
import jax.numpy as jnp
from jax import lax
from jax.experimental import pallas as pl
from jax.experimental.pallas import tpu as pltpu
from jax.sharding import PartitionSpec as P

GROUPS = 32
DILATION_FRAMES = 4


epsilon = 1e-05


def delay_rows(values):
    return jnp.pad(values, ((0, 0), (1, 0), (0, 0), (0, 0)))[:, :-1]


def delay_cols(values):
    return jnp.pad(values, ((0, 0), (0, 0), (1, 0), (0, 0)))[:, :, :-1]


def advance_rows(values):
    return jnp.pad(values, ((0, 0), (0, 1), (0, 0), (0, 0)))[:, 1:]


def advance_cols(values):
    return jnp.pad(values, ((0, 0), (0, 0), (0, 1), (0, 0)))[:, :, 1:]


def split_phases(frames_in):
    frames, height, width, chans = frames_in.shape
    viewed = frames_in.reshape(frames, height // 2, 2, width // 2, 2, chans)
    phases = {}
    for row_phase in range(2):
        for col_phase in range(2):
            phases[row_phase, col_phase] = viewed[:, :, row_phase, :, col_phase, :].reshape(
                -1, chans
            )
    return phases


def tap_layout(offset):
    return (0 if offset == 1 else 1, offset == 0)


def membership(chans):
    channel_group = lax.broadcasted_iota(jnp.int32, (chans, GROUPS), 0) // (chans // GROUPS)
    group_index = lax.broadcasted_iota(jnp.int32, (chans, GROUPS), 1)
    return (channel_group == group_index).astype(jnp.float32)


def activate(conv_out, gain, bias):
    chans = conv_out.shape[-1]
    member = membership(chans)
    count = conv_out.shape[1] * conv_out.shape[2] * (chans // GROUPS)
    high = lax.Precision.HIGHEST
    chan_sum = jnp.sum(conv_out, axis=(1, 2))
    group_mean = jnp.dot(chan_sum, member, precision=high) / count
    center = jnp.dot(group_mean, member.T, precision=high)
    deviation = conv_out - center[:, None, None, :]
    chan_square = jnp.sum(deviation * deviation, axis=(1, 2))
    group_var = jnp.dot(chan_square, member, precision=high) / count
    scaling = jnp.dot(lax.rsqrt(group_var + epsilon), member.T, precision=high)
    normed = deviation * scaling[:, None, None, :]
    return jax.nn.silu(normed * gain + bias)


def from_device(values, offset, tm_size):
    pairs = [(src, src + offset) for src in range(tm_size) if 0 <= src + offset < tm_size]
    return lax.ppermute(values, "tm", pairs)


def index_groups(clip_size, tm_size):
    clip_bits = [1 << k for k in range(clip_size.bit_length() - 1)]
    tm_bits = [1 << k for k in range(tm_size.bit_length() - 1)]
    groups = [("clip", clip_bits[:1])] if clip_bits else []
    groups += [("tm", tm_bits[k : k + 2]) for k in range(0, len(tm_bits), 2)]
    groups += [("clip", clip_bits[k : k + 2]) for k in range(1, len(clip_bits), 2)]
    return groups


STREAMS = 2


def sum_kernel(groups, sizes, *refs):
    parts, refs = refs[: len(sizes)], refs[len(sizes) :]
    out_ref, acc, outgoing, incoming, rs_send, rs_recv, ag_send, ag_recv = refs
    place = {"clip": lax.axis_index("clip"), "tm": lax.axis_index("tm")}
    digits, peers = [], []
    for axis, weights in groups:
        bits = [(place[axis] // weight) % 2 for weight in weights]
        digits.append(sum(bit * (1 << k) for k, bit in enumerate(bits)))
        members = []
        for flip in range(1, 1 << len(weights)):
            other, digit = place[axis], 0
            for k, weight in enumerate(weights):
                flipped = (flip >> k) & 1
                other = other + flipped * weight * (1 - 2 * bits[k])
                digit = digit + (1 << k) * (1 - bits[k] if flipped else bits[k])
            device = (other, place["tm"]) if axis == "clip" else (place["clip"], other)
            members.append((device, digit))
        peers.append(members)

    barrier = pltpu.get_barrier_semaphore()
    for members in peers:
        for device, _ in members:
            pl.semaphore_signal(
                barrier, inc=1, device_id=device, device_id_type=pl.DeviceIdType.MESH
            )

    _, devices, unit, chans = acc.shape
    flat = acc.reshape(STREAMS * devices * unit, chans)
    row = 0
    for part, size in zip(parts, sizes):
        flat[row : row + size] = part[...].reshape(size, chans)
        row += size
    flat[row:] = jnp.zeros((flat.shape[0] - row, chans), jnp.float32)
    pl.semaphore_wait(barrier, sum(len(members) for members in peers))

    count = len(groups)
    orders = [list(range(count)) for _ in range(STREAMS)]
    if count > 2:
        orders[1][1], orders[1][2] = 2, 1
    pieces, slots = [], []
    for order in orders:
        size, slot = devices, 0
        pieces.append([])
        slots.append([])
        for which in order:
            size //= len(peers[which]) + 1
            pieces[-1].append(size)
            slots[-1].append(slot)
            slot += size * len(peers[which])
    base = [0] * STREAMS
    kept = [[] for _ in range(STREAMS)]
    flying = [[] for _ in range(STREAMS)]
    copies = []

    def send(stream, turn, index, source, target, sems):
        which = orders[stream][turn]
        sem = sum(len(members) for members in peers[:which]) + index
        copy = pltpu.make_async_remote_copy(
            src_ref=source,
            dst_ref=target,
            send_sem=sems[0].at[stream, sem],
            recv_sem=sems[1].at[stream, sem],
            device_id=peers[which][index][0],
            device_id_type=pl.DeviceIdType.MESH,
        )
        copy.start()
        copies.append(copy)
        flying[stream].append(copy)

    def send_pieces(stream, turn):
        size = pieces[stream][turn]
        flying[stream] = []
        for index, (_, digit) in enumerate(peers[orders[stream][turn]]):
            slot = pl.ds(slots[stream][turn] + index * size, size)
            give = pl.ds(base[stream] + digit * size, size)
            outgoing[stream, slot] = acc[stream, give].astype(jnp.bfloat16)
            send(
                stream,
                turn,
                index,
                outgoing.at[stream, slot],
                incoming.at[stream, slot],
                (rs_send, rs_recv),
            )

    def add_pieces(stream, turn):
        which = orders[stream][turn]
        size = pieces[stream][turn]
        base[stream] = base[stream] + digits[which] * size
        keep = pl.ds(base[stream], size)
        for copy in flying[stream]:
            copy.wait_recv()
        total = acc[stream, keep]
        for index in range(len(peers[which])):
            slot = pl.ds(slots[stream][turn] + index * size, size)
            total = total + incoming[stream, slot].astype(jnp.float32)
        acc[stream, keep] = total
        kept[stream].append(base[stream])

    def send_held(stream, turn):
        held = out_ref.at[stream, pl.ds(kept[stream][turn], pieces[stream][turn])]
        flying[stream] = []
        for index in range(len(peers[orders[stream][turn]])):
            send(stream, turn, index, held, held, (ag_send, ag_recv))

    for stream in range(STREAMS):
        send_pieces(stream, 0)
    for turn in range(count):
        for stream in range(STREAMS):
            add_pieces(stream, turn)
            if turn + 1 < count:
                send_pieces(stream, turn + 1)
            else:
                own = pl.ds(base[stream], 1)
                out_ref[stream, own] = acc[stream, own].astype(jnp.bfloat16)
                send_held(stream, turn)
    for turn in reversed(range(count)):
        for stream in range(STREAMS):
            for copy in flying[stream]:
                copy.wait_recv()
            if turn > 0:
                send_held(stream, turn - 1)
    for copy in copies:
        copy.wait_send()


def sum_everywhere(parts, clip_size, tm_size):
    devices = clip_size * tm_size
    groups = index_groups(clip_size, tm_size)
    exchanges = sum((1 << len(weights)) - 1 for _, weights in groups)
    chans = parts[0].shape[-1]
    sizes = tuple(part.shape[0] for part in parts)
    unit = -(-sum(sizes) // (STREAMS * devices * 8)) * 8
    shape = (STREAMS, devices, unit, chans)
    total = pl.pallas_call(
        functools.partial(sum_kernel, groups, sizes),
        out_shape=jax.ShapeDtypeStruct(shape, jnp.bfloat16),
        in_specs=[pl.BlockSpec(memory_space=pltpu.VMEM)] * len(parts),
        out_specs=pl.BlockSpec(memory_space=pltpu.VMEM),
        scratch_shapes=[
            pltpu.VMEM(shape, jnp.float32),
            pltpu.VMEM(shape, jnp.bfloat16),
            pltpu.VMEM(shape, jnp.bfloat16),
        ]
        + [pltpu.SemaphoreType.DMA((STREAMS, exchanges))] * 4,
        compiler_params=pltpu.CompilerParams(
            collective_id=0, has_side_effects=True, vmem_limit_bytes=32 * 1024 * 1024
        ),
    )(*parts)
    return total.reshape(-1, chans).astype(jnp.float32)


def later_frames(upstream, hop, tm_size):
    upper = (lax.axis_index("tm") // hop) % 2 == 1
    lows = [place for place in range(tm_size) if place // hop % 2 == 0]
    far = [from_device(block, -2 * hop, tm_size) for block in upstream]
    own = lax.ppermute(upstream, "tm", [(low + hop, low) for low in lows])
    passed = [lax.ppermute(block, "tm", [(low, low + hop) for low in lows]) for block in far]
    near = [jnp.where(upper, passed[k], own[k]) for k in range(len(far))]
    return jnp.stack(near), jnp.stack(far)


def per_device(clip_size, tm_size, clip_frames, spatial_weight, norm_gain, norm_bias, temporal_weight, cotangent):
    frames_in = clip_frames[0]
    upstream = cotangent[0]
    frames, height, width, _ = frames_in.shape
    out_chans = spatial_weight.shape[-1]
    out_shape = (frames, height // 2, width // 2, out_chans)
    phases = split_phases(frames_in)
    partial_sums = {}
    for row_offset in range(3):
        row_phase, row_delay = tap_layout(row_offset)
        for col_offset in range(3):
            col_phase, col_delay = tap_layout(col_offset)
            product = jnp.dot(
                phases[row_phase, col_phase],
                spatial_weight[row_offset, col_offset],
                preferred_element_type=jnp.float32,
            )
            key_pair = (row_delay, col_delay)
            if key_pair in partial_sums:
                partial_sums[key_pair] = partial_sums[key_pair] + product
            else:
                partial_sums[key_pair] = product
    conv_out = partial_sums[False, False].reshape(out_shape)
    conv_out = conv_out + delay_rows(partial_sums[True, False].reshape(out_shape))
    conv_out = conv_out + delay_cols(partial_sums[False, True].reshape(out_shape))
    conv_out = conv_out + delay_rows(delay_cols(partial_sums[True, True].reshape(out_shape)))
    activated, pullback = jax.vjp(activate, conv_out, norm_gain, norm_bias)
    acts = activated.astype(jnp.bfloat16)
    flat_acts = acts.reshape(-1, out_chans)
    mixed_sum = flat_acts.astype(jnp.float32)
    act_grad_sum = upstream.reshape(-1, out_chans).astype(jnp.float32)
    tap_grads = []
    hop = DILATION_FRAMES // frames
    near, far = later_frames(upstream, hop, tm_size)
    far_acts = from_device(acts, 2 * hop, tm_size)
    upstream, near, far, far_acts = lax.optimization_barrier((upstream, near, far, far_acts))
    upper = (lax.axis_index("tm") // hop) % 2 == 1
    near_acts = lax.ppermute(
        jnp.where(upper, far_acts, acts), "tm", [(src, src ^ hop) for src in range(tm_size)]
    )
    for tap in range(3):
        earlier = (acts, near_acts, far_acts)[tap]
        later = (upstream, near, far)[tap]
        earlier = earlier.reshape(-1, out_chans)
        later = later.reshape(-1, out_chans)
        mixed_sum = mixed_sum + jnp.dot(
            earlier, temporal_weight[tap], preferred_element_type=jnp.float32
        )
        act_grad_sum = act_grad_sum + jnp.dot(
            later, temporal_weight[tap].T, preferred_element_type=jnp.float32
        )
        tap_grads.append(
            lax.dot_general(
                flat_acts, later, (((0,), (0,)), ((), ())), preferred_element_type=jnp.float32
            )
        )
    mixed = mixed_sum.astype(jnp.bfloat16).reshape(out_shape)
    act_grad = act_grad_sum.astype(jnp.bfloat16).reshape(out_shape)
    conv_grad, gain_partial_sum, bias_part = pullback(act_grad.astype(jnp.float32))
    conv_grad = conv_grad.astype(jnp.bfloat16)
    grad_versions = {
        (False, False): conv_grad.reshape(-1, out_chans),
        (True, False): advance_rows(conv_grad).reshape(-1, out_chans),
        (False, True): advance_cols(conv_grad).reshape(-1, out_chans),
        (True, True): advance_rows(advance_cols(conv_grad)).reshape(-1, out_chans),
    }
    parts = []
    for row_offset in range(3):
        row_phase, row_delay = tap_layout(row_offset)
        for col_offset in range(3):
            col_phase, col_delay = tap_layout(col_offset)
            parts.append(
                lax.dot_general(
                    phases[row_phase, col_phase],
                    grad_versions[row_delay, col_delay],
                    (((0,), (0,)), ((), ())),
                    preferred_element_type=jnp.float32,
                )
            )
    spatial_rows = 9 * spatial_weight.shape[2]
    parts += tap_grads
    parts.append(jnp.stack([gain_partial_sum, bias_part]))
    totals = sum_everywhere(parts, clip_size, tm_size)
    spatial_gradient_total = totals[:spatial_rows].reshape(spatial_weight.shape)
    temporal_total = totals[spatial_rows : spatial_rows + 3 * out_chans].reshape(
        temporal_weight.shape
    )
    gain_total = totals[spatial_rows + 3 * out_chans]
    bias_total = totals[spatial_rows + 3 * out_chans + 1]
    return (mixed[None], spatial_gradient_total, gain_total, bias_total, temporal_total)


def solution(mesh):
    return jax.shard_map(
        functools.partial(per_device, mesh.shape["clip"], mesh.shape["tm"]),
        mesh=mesh,
        in_specs=(
            P("clip", "tm", None, None, None),
            P(),
            P(),
            P(),
            P(),
            P("clip", "tm", None, None, None),
        ),
        out_specs=(P("clip", "tm", None, None, None), P(), P(), P(), P()),
        check_vma=False,
    )
```

```python
import functools

import jax
import jax.numpy as jnp
from jax import lax
from jax.experimental import pallas as pl
from jax.experimental.pallas import tpu as pltpu
from jax.sharding import PartitionSpec as P

GROUPS = 32
DILATION_FRAMES = 4


epsilon = 1e-05


def delay_rows(values):
    return jnp.pad(values, ((0, 0), (1, 0), (0, 0), (0, 0)))[:, :-1]


def delay_cols(values):
    return jnp.pad(values, ((0, 0), (0, 0), (1, 0), (0, 0)))[:, :, :-1]


def advance_rows(values):
    return jnp.pad(values, ((0, 0), (0, 1), (0, 0), (0, 0)))[:, 1:]


def advance_cols(values):
    return jnp.pad(values, ((0, 0), (0, 0), (0, 1), (0, 0)))[:, :, 1:]


def split_phases(frames_in):
    frames, height, width, chans = frames_in.shape
    viewed = frames_in.reshape(frames, height // 2, 2, width // 2, 2, chans)
    phases = {}
    for row_phase in range(2):
        for col_phase in range(2):
            phases[row_phase, col_phase] = viewed[:, :, row_phase, :, col_phase, :].reshape(
                -1, chans
            )
    return phases


def tap_layout(offset):
    return (0 if offset == 1 else 1, offset == 0)


def membership(chans):
    channel_group = lax.broadcasted_iota(jnp.int32, (chans, GROUPS), 0) // (chans // GROUPS)
    group_index = lax.broadcasted_iota(jnp.int32, (chans, GROUPS), 1)
    return (channel_group == group_index).astype(jnp.float32)


def activate(conv_out, gain, bias):
    chans = conv_out.shape[-1]
    member = membership(chans)
    count = conv_out.shape[1] * conv_out.shape[2] * (chans // GROUPS)
    high = lax.Precision.HIGHEST
    chan_sum = jnp.sum(conv_out, axis=(1, 2))
    group_mean = jnp.dot(chan_sum, member, precision=high) / count
    center = jnp.dot(group_mean, member.T, precision=high)
    deviation = conv_out - center[:, None, None, :]
    chan_square = jnp.sum(deviation * deviation, axis=(1, 2))
    group_var = jnp.dot(chan_square, member, precision=high) / count
    scaling = jnp.dot(lax.rsqrt(group_var + epsilon), member.T, precision=high)
    normed = deviation * scaling[:, None, None, :]
    return jax.nn.silu(normed * gain + bias)


def from_device(values, offset, tm_size):
    pairs = [(src, src + offset) for src in range(tm_size) if 0 <= src + offset < tm_size]
    return lax.ppermute(values, "tm", pairs)


def index_groups(clip_size, tm_size):
    clip_bits = [1 << k for k in range(clip_size.bit_length() - 1)]
    tm_bits = [1 << k for k in range(tm_size.bit_length() - 1)]
    groups = [("clip", clip_bits[:1])] if clip_bits else []
    groups += [("tm", tm_bits[k : k + 2]) for k in range(0, len(tm_bits), 2)]
    groups += [("clip", clip_bits[k : k + 2]) for k in range(1, len(clip_bits), 2)]
    return groups


STREAMS = 4


def sum_kernel(groups, sizes, *refs):
    parts, refs = refs[: len(sizes)], refs[len(sizes) :]
    out_ref, acc, outgoing, incoming, rs_send, rs_recv, ag_send, ag_recv = refs
    place = {"clip": lax.axis_index("clip"), "tm": lax.axis_index("tm")}
    digits, peers = [], []
    for axis, weights in groups:
        bits = [(place[axis] // weight) % 2 for weight in weights]
        digits.append(sum(bit * (1 << k) for k, bit in enumerate(bits)))
        members = []
        for flip in range(1, 1 << len(weights)):
            other, digit = place[axis], 0
            for k, weight in enumerate(weights):
                flipped = (flip >> k) & 1
                other = other + flipped * weight * (1 - 2 * bits[k])
                digit = digit + (1 << k) * (1 - bits[k] if flipped else bits[k])
            device = (other, place["tm"]) if axis == "clip" else (place["clip"], other)
            members.append((device, digit))
        peers.append(members)

    barrier = pltpu.get_barrier_semaphore()
    for members in peers:
        for device, _ in members:
            pl.semaphore_signal(
                barrier, inc=1, device_id=device, device_id_type=pl.DeviceIdType.MESH
            )

    _, devices, unit, chans = acc.shape
    flat = acc.reshape(STREAMS * devices * unit, chans)
    row = 0
    for part, size in zip(parts, sizes):
        flat[row : row + size] = part[...].reshape(size, chans)
        row += size
    flat[row:] = jnp.zeros((flat.shape[0] - row, chans), jnp.float32)
    pl.semaphore_wait(barrier, sum(len(members) for members in peers))

    count = len(groups)
    orders = [list(range(count)) for _ in range(STREAMS)]
    if count > 2:
        for order in orders[1::2]:
            order[1], order[2] = 2, 1
    pieces, slots = [], []
    for order in orders:
        size, slot = devices, 0
        pieces.append([])
        slots.append([])
        for which in order:
            size //= len(peers[which]) + 1
            pieces[-1].append(size)
            slots[-1].append(slot)
            slot += size * len(peers[which])
    base = [0] * STREAMS
    kept = [[] for _ in range(STREAMS)]
    flying = [[] for _ in range(STREAMS)]
    copies = []

    def send(stream, turn, index, source, target, sems):
        which = orders[stream][turn]
        sem = sum(len(members) for members in peers[:which]) + index
        copy = pltpu.make_async_remote_copy(
            src_ref=source,
            dst_ref=target,
            send_sem=sems[0].at[stream, sem],
            recv_sem=sems[1].at[stream, sem],
            device_id=peers[which][index][0],
            device_id_type=pl.DeviceIdType.MESH,
        )
        copy.start()
        copies.append(copy)
        flying[stream].append(copy)

    def send_pieces(stream, turn):
        size = pieces[stream][turn]
        flying[stream] = []
        for index, (_, digit) in enumerate(peers[orders[stream][turn]]):
            slot = pl.ds(slots[stream][turn] + index * size, size)
            give = pl.ds(base[stream] + digit * size, size)
            outgoing[stream, slot] = acc[stream, give].astype(jnp.bfloat16)
            send(
                stream,
                turn,
                index,
                outgoing.at[stream, slot],
                incoming.at[stream, slot],
                (rs_send, rs_recv),
            )

    def add_pieces(stream, turn):
        which = orders[stream][turn]
        size = pieces[stream][turn]
        base[stream] = base[stream] + digits[which] * size
        keep = pl.ds(base[stream], size)
        for copy in flying[stream]:
            copy.wait_recv()
        total = acc[stream, keep]
        for index in range(len(peers[which])):
            slot = pl.ds(slots[stream][turn] + index * size, size)
            total = total + incoming[stream, slot].astype(jnp.float32)
        acc[stream, keep] = total
        kept[stream].append(base[stream])

    def send_held(stream, turn):
        held = out_ref.at[stream, pl.ds(kept[stream][turn], pieces[stream][turn])]
        flying[stream] = []
        for index in range(len(peers[orders[stream][turn]])):
            send(stream, turn, index, held, held, (ag_send, ag_recv))

    for stream in range(STREAMS):
        send_pieces(stream, 0)
    for turn in range(count):
        for stream in range(STREAMS):
            add_pieces(stream, turn)
            if turn + 1 < count:
                send_pieces(stream, turn + 1)
            else:
                own = pl.ds(base[stream], 1)
                out_ref[stream, own] = acc[stream, own].astype(jnp.bfloat16)
                send_held(stream, turn)
    for turn in reversed(range(count)):
        for stream in range(STREAMS):
            for copy in flying[stream]:
                copy.wait_recv()
            if turn > 0:
                send_held(stream, turn - 1)
    for copy in copies:
        copy.wait_send()


def sum_everywhere(parts, clip_size, tm_size):
    devices = clip_size * tm_size
    groups = index_groups(clip_size, tm_size)
    exchanges = sum((1 << len(weights)) - 1 for _, weights in groups)
    chans = parts[0].shape[-1]
    sizes = tuple(part.shape[0] for part in parts)
    unit = -(-sum(sizes) // (STREAMS * devices * 8)) * 8
    shape = (STREAMS, devices, unit, chans)
    total = pl.pallas_call(
        functools.partial(sum_kernel, groups, sizes),
        out_shape=jax.ShapeDtypeStruct(shape, jnp.bfloat16),
        in_specs=[pl.BlockSpec(memory_space=pltpu.VMEM)] * len(parts),
        out_specs=pl.BlockSpec(memory_space=pltpu.VMEM),
        scratch_shapes=[
            pltpu.VMEM(shape, jnp.float32),
            pltpu.VMEM(shape, jnp.bfloat16),
            pltpu.VMEM(shape, jnp.bfloat16),
        ]
        + [pltpu.SemaphoreType.DMA((STREAMS, exchanges))] * 4,
        compiler_params=pltpu.CompilerParams(
            collective_id=0, has_side_effects=True, vmem_limit_bytes=32 * 1024 * 1024
        ),
    )(*parts)
    return total.reshape(-1, chans).astype(jnp.float32)


def later_frames(upstream, hop, tm_size):
    upper = (lax.axis_index("tm") // hop) % 2 == 1
    lows = [place for place in range(tm_size) if place // hop % 2 == 0]
    far = [from_device(block, -2 * hop, tm_size) for block in upstream]
    own = lax.ppermute(upstream, "tm", [(low + hop, low) for low in lows])
    passed = [lax.ppermute(block, "tm", [(low, low + hop) for low in lows]) for block in far]
    near = [jnp.where(upper, passed[k], own[k]) for k in range(len(far))]
    return jnp.stack(near), jnp.stack(far)


def per_device(clip_size, tm_size, clip_frames, spatial_weight, norm_gain, norm_bias, temporal_weight, cotangent):
    frames_in = clip_frames[0]
    upstream = cotangent[0]
    frames, height, width, _ = frames_in.shape
    out_chans = spatial_weight.shape[-1]
    out_shape = (frames, height // 2, width // 2, out_chans)
    phases = split_phases(frames_in)
    partial_sums = {}
    for row_offset in range(3):
        row_phase, row_delay = tap_layout(row_offset)
        for col_offset in range(3):
            col_phase, col_delay = tap_layout(col_offset)
            product = jnp.dot(
                phases[row_phase, col_phase],
                spatial_weight[row_offset, col_offset],
                preferred_element_type=jnp.float32,
            )
            key_pair = (row_delay, col_delay)
            if key_pair in partial_sums:
                partial_sums[key_pair] = partial_sums[key_pair] + product
            else:
                partial_sums[key_pair] = product
    conv_out = partial_sums[False, False].reshape(out_shape)
    conv_out = conv_out + delay_rows(partial_sums[True, False].reshape(out_shape))
    conv_out = conv_out + delay_cols(partial_sums[False, True].reshape(out_shape))
    conv_out = conv_out + delay_rows(delay_cols(partial_sums[True, True].reshape(out_shape)))
    activated, pullback = jax.vjp(activate, conv_out, norm_gain, norm_bias)
    acts = activated.astype(jnp.bfloat16)
    flat_acts = acts.reshape(-1, out_chans)
    mixed_sum = flat_acts.astype(jnp.float32)
    act_grad_sum = upstream.reshape(-1, out_chans).astype(jnp.float32)
    tap_grads = []
    hop = DILATION_FRAMES // frames
    near, far = later_frames(upstream, hop, tm_size)
    far_acts = from_device(acts, 2 * hop, tm_size)
    upstream, near, far, far_acts = lax.optimization_barrier((upstream, near, far, far_acts))
    upper = (lax.axis_index("tm") // hop) % 2 == 1
    near_acts = lax.ppermute(
        jnp.where(upper, far_acts, acts), "tm", [(src, src ^ hop) for src in range(tm_size)]
    )
    for tap in range(3):
        earlier = (acts, near_acts, far_acts)[tap]
        later = (upstream, near, far)[tap]
        earlier = earlier.reshape(-1, out_chans)
        later = later.reshape(-1, out_chans)
        mixed_sum = mixed_sum + jnp.dot(
            earlier, temporal_weight[tap], preferred_element_type=jnp.float32
        )
        act_grad_sum = act_grad_sum + jnp.dot(
            later, temporal_weight[tap].T, preferred_element_type=jnp.float32
        )
        tap_grads.append(
            lax.dot_general(
                flat_acts, later, (((0,), (0,)), ((), ())), preferred_element_type=jnp.float32
            )
        )
    mixed = mixed_sum.astype(jnp.bfloat16).reshape(out_shape)
    act_grad = act_grad_sum.astype(jnp.bfloat16).reshape(out_shape)
    conv_grad, gain_partial_sum, bias_part = pullback(act_grad.astype(jnp.float32))
    conv_grad = conv_grad.astype(jnp.bfloat16)
    grad_versions = {
        (False, False): conv_grad.reshape(-1, out_chans),
        (True, False): advance_rows(conv_grad).reshape(-1, out_chans),
        (False, True): advance_cols(conv_grad).reshape(-1, out_chans),
        (True, True): advance_rows(advance_cols(conv_grad)).reshape(-1, out_chans),
    }
    parts = []
    for row_offset in range(3):
        row_phase, row_delay = tap_layout(row_offset)
        for col_offset in range(3):
            col_phase, col_delay = tap_layout(col_offset)
            parts.append(
                lax.dot_general(
                    phases[row_phase, col_phase],
                    grad_versions[row_delay, col_delay],
                    (((0,), (0,)), ((), ())),
                    preferred_element_type=jnp.float32,
                )
            )
    spatial_rows = 9 * spatial_weight.shape[2]
    parts += tap_grads
    parts.append(jnp.stack([gain_partial_sum, bias_part]))
    totals = sum_everywhere(parts, clip_size, tm_size)
    spatial_gradient_total = totals[:spatial_rows].reshape(spatial_weight.shape)
    temporal_total = totals[spatial_rows : spatial_rows + 3 * out_chans].reshape(
        temporal_weight.shape
    )
    gain_total = totals[spatial_rows + 3 * out_chans]
    bias_total = totals[spatial_rows + 3 * out_chans + 1]
    return (mixed[None], spatial_gradient_total, gain_total, bias_total, temporal_total)


def solution(mesh):
    return jax.shard_map(
        functools.partial(per_device, mesh.shape["clip"], mesh.shape["tm"]),
        mesh=mesh,
        in_specs=(
            P("clip", "tm", None, None, None),
            P(),
            P(),
            P(),
            P(),
            P("clip", "tm", None, None, None),
        ),
        out_specs=(P("clip", "tm", None, None, None), P(), P(), P(), P()),
        check_vma=False,
    )
```
